512 devices in a mesh: wide: 32 (over x, y), grp: 16 (over z, core).
Axes of the slice: x: 4, y: 8, z: 8, core: 2. Of those that a mesh axis runs over, the one named last changes fastest.
Arguments:
- amplitudes: bfloat16 [128, 128, 256, 256], P(None, 'wide', 'grp'), may hold values from -6 to 6
- integrals: bfloat16 [4, 128, 256, 256], P(None, 'grp', 'wide'), may hold values from -0.0625 to 0.0625
- pair_local: int32 [4, 128], replicated, may hold values from 0 to 1, as said below
Outputs:
- cycle_term: bfloat16 [4, 128, 256, 256], P(None, 'wide', 'grp')
The draws below stay inside these ranges and needn't reach their ends.
Inputs may be any that keep to these rules, and one draw needn't show every extreme that they name: `pair_local`: 1 marks a pair (i, k) of occupied orbitals inside the locality domain, 0 a screened pair.
All inputs are finite; a program needn't handle non-finite values.
Results may differ from the reference program's by a relative error of at most 0.001.
Values may be sent and summed in bfloat16 or wider, within the bound.
No kernel may reach another device: no remote copies, remote signals or barrier semaphores. Data moves between devices by JAX's collectives and lax.ppermute only.
A program may use at most 128 MiB of HBM per device.

```python
import jax
import jax.numpy as jnp
from jax import lax

V = 256
I_ROWS = 4
OCC = 128
J_ALL = 128


def draw_pair_local(key, part):
    rolled = jax.random.randint(key, (I_ROWS, OCC), 0, 4 * OCC)
    columns = jnp.arange(OCC, dtype=jnp.int32)[None, :]
    row_index = jnp.arange(I_ROWS, dtype=jnp.int32)[:, None]
    inside = (rolled < OCC + 3 * columns) | (columns % I_ROWS == row_index)
    return inside.astype(jnp.int32)


def raised(array, own_key, source, target, blocks, factor):
    def block_of(dim):
        return (jnp.arange(array.shape[dim]) // (array.shape[dim] // blocks)).reshape((-1,) + (1,) * (array.ndim - 1 - dim))

    first = jax.random.permutation(own_key, blocks)[block_of(target)]
    far = (block_of(target) + blocks // 2) % blocks
    return jnp.where((block_of(source) == first) | (block_of(source) == far), factor * array, array)


def steps_of(own_key, extent, shards, smallest, high):
    gain, own = 1.0, jax.random.fold_in(own_key, 6)
    for axis_at, blocks in shards:
        draws = jnp.exp(jax.random.uniform(jax.random.fold_in(own, axis_at), (blocks,), jnp.float32, smallest / len(shards), high / len(shards)))
        gain = gain * jnp.repeat(draws, extent[axis_at] // blocks).reshape([-1 if axis == axis_at else 1 for axis in range(len(extent))])
    return gain


def normal_values(rng, dims, width, bound, split=(), held_as=jnp.bfloat16):
    factor_of = steps_of(rng, dims, split, -0.22, 0.18) if split else 1.0
    entries = jax.random.normal(rng, dims, jnp.float32) * width * factor_of
    return jnp.minimum(jnp.maximum(entries, -bound), bound).astype(held_as)


def heavy_noise(key, extent, scale, bound, split, heavy, held_as=jnp.bfloat16):
    drawn = scale * jax.random.normal(key, extent, jnp.float32)
    if split:
        drawn = drawn * steps_of(key, extent, split, -0.22, 0.18)
    return jnp.clip(raised(drawn, jax.random.fold_in(key, 3), *heavy), -bound, bound).astype(held_as)


def setup_inputs(seed: int = 0) -> dict:
    splits = jax.random.split(jax.random.key(seed), 4)
    return {
        "amplitudes": normal_values(splits[0], (OCC, J_ALL, V, V), 1.0, 6.0, ((1, 32), (2, 16))),
        "integrals": heavy_noise(splits[1], (I_ROWS, OCC, V, V), (OCC * V) ** -0.5, 0.0625, ((1, 16), (2, 32)), (1, 2, 32, 2.75)),
        "pair_local": draw_pair_local(jax.random.fold_in(splits[3], 71), 0),
    }


def reference(amplitudes, integrals, pair_local):
    factor = pair_local.astype(jnp.bfloat16)[:, :, None, None]
    masked = integrals * factor
    row_matrix = jnp.transpose(masked, (0, 2, 1, 3)).reshape(I_ROWS * V, OCC * V)

    def column(column_index):
        column_block = lax.dynamic_index_in_dim(amplitudes, column_index, 1, keepdims=False)
        column_block = column_block.reshape(OCC * V, V)
        return jnp.dot(row_matrix, column_block, preferred_element_type=jnp.float32).astype(jnp.bfloat16)

    stacked = lax.map(column, jnp.arange(J_ALL, dtype=jnp.int32))
    stacked = stacked.reshape(J_ALL, I_ROWS, V, V)
    return jnp.transpose(stacked, (1, 0, 2, 3))
```

```python
import jax
import jax.numpy as jnp
from jax import lax
from jax.experimental import pallas as pl
from jax.experimental.pallas import tpu as pltpu
from jax.sharding import Mesh, PartitionSpec as P

BF16, F16, F32 = jnp.bfloat16, jnp.float16, jnp.float32
LADDER = (64, 32, 16, 8, 4, 2, 1)


def raise_to_range(peak):
    peak = jnp.maximum(peak, 2.0**-100)
    scale, power = jnp.ones_like(peak), jnp.zeros_like(peak)
    for step in LADDER:
        fits = peak * scale <= 2.0 ** (15 - step)
        scale = jnp.where(fits, scale * 2.0**step, scale)
        power = jnp.where(fits, power + step, power)
    return scale, power


def lower_again(power):
    scale, left = jnp.ones_like(power), power
    for step in LADDER:
        take = left >= step
        scale = jnp.where(take, scale * 2.0**-step, scale)
        left = jnp.where(take, left - step, left)
    return scale


def product_kernel(inverse_ref, w_ref, t_ref, out_ref):
    pair = pl.program_id(1)
    rows = jnp.concatenate(
        [w_ref[:, :, g].reshape(256, 128) for g in range(16)], axis=1
    )
    columns = t_ref[:, 0].reshape(2048, 256)
    acc = jnp.dot(rows, columns, preferred_element_type=F32).reshape(2, 4, 32, 256)
    for half in range(2):
        out_ref[0, :, 0, half] = acc[half] * inverse_ref[2 * pair + half]


def product(inverse, w, t):
    return pl.pallas_call(
        product_kernel,
        grid_spec=pltpu.PrefetchScalarGridSpec(
            num_scalar_prefetch=1,
            grid=(4, 4),
            in_specs=[
                pl.BlockSpec((2, 4, 16, 32, 128), lambda j, m, s: (m, 0, 0, 0, 0)),
                pl.BlockSpec((128, 1, 16, 256), lambda j, m, s: (0, j, 0, 0)),
            ],
            out_specs=pl.BlockSpec(
                (1, 4, 1, 2, 32, 256), lambda j, m, s: (m % 2, 0, m // 2, 0, 0, j)
            ),
        ),
        out_shape=jax.ShapeDtypeStruct((2, 4, 2, 2, 32, 1024), F32),
        cost_estimate=pl.CostEstimate(
            flops=2 * 1024 * 2048 * 1024, bytes_accessed=12 << 20, transcendentals=0
        ),
    )(inverse, w, t)


def body(amplitudes, integrals, pair_local):
    group = lax.axis_index(("z", "core"))
    weights = lax.dynamic_slice_in_dim(pair_local, group * 8, 8, 1)
    masked = integrals * weights.astype(BF16)[:, :, None, None]
    pieces = masked.reshape(4, 8, 8, 16, 16).transpose(3, 0, 2, 1, 4).reshape(16, 32, 128)
    pieces = jnp.broadcast_to(pieces[None], (4, 16, 32, 128)).reshape(64, 32, 128)
    block = lax.all_to_all(pieces, ("x", "z", "core"), 0, 0, tiled=True)
    block = block.reshape(2048, 128).astype(F32)
    scale, power = raise_to_range(jnp.max(jnp.abs(block)))
    sent = jnp.concatenate(
        [(block * scale).astype(F16), jnp.broadcast_to(power.astype(F16), (16, 128))]
    )
    gathered = lax.all_gather(sent, "y", axis=0)
    inverse = lower_again(gathered[:, 2048, 0].astype(F32))
    w = gathered[:, :2048].astype(BF16).reshape(8, 4, 16, 32, 128)
    part = product(inverse, w, amplitudes).reshape(2, 512, 1024)
    both = lax.all_to_all(part, "core", 0, 0, tiled=True)
    chip = (both[0] + both[1]).reshape(8, 64, 1024)
    shares = lax.all_to_all(chip, "z", 0, 0, tiled=True)
    total = jnp.sum(shares, axis=0).astype(BF16)
    total = total.reshape(2, 4, 8, 4, 256).transpose(1, 3, 0, 2, 4)
    return total.reshape(4, 4, 16, 256)


def solution(mesh):
    chips = Mesh(mesh.devices.reshape(4, 8, 8, 2), ("x", "y", "z", "core"))
    wide, grp = ("x", "y"), ("z", "core")
    in_specs = (P(None, wide, grp, None), P(None, grp, wide, None), P())
    out_specs = P(None, wide, grp, None)
    return jax.shard_map(body, mesh=chips, in_specs=in_specs, out_specs=out_specs, check_vma=False)
```

```python
import jax
import jax.numpy as jnp
from jax import lax
from jax.experimental import pallas as pl
from jax.experimental.pallas import tpu as pltpu
from jax.sharding import Mesh, PartitionSpec as P

BF16, F16, F32, I16, I32 = jnp.bfloat16, jnp.float16, jnp.float32, jnp.int16, jnp.int32
LADDER = (64, 32, 16, 8, 4, 2, 1)
X, Y, Z = 4, 8, 8
CHUNKS = ((0, 4),)
FULL = 2.0**14 * 1.875


def raise_to_range(peak):
    peak = jnp.maximum(peak, 2.0**-100)
    scale, power = jnp.ones_like(peak), jnp.zeros_like(peak)
    for step in LADDER:
        fits = peak * scale <= 2.0 ** (15 - step)
        scale = jnp.where(fits, scale * 2.0**step, scale)
        power = jnp.where(fits, power + step, power)
    return scale, power


def lower_again(power):
    scale, left = jnp.ones_like(power), power
    for step in LADDER:
        take = left >= step
        scale = jnp.where(take, scale * 2.0**-step, scale)
        left = jnp.where(take, left - step, left)
    return scale


def code_kernel(own_ref, other_ref, out_ref):
    blocks = own_ref.shape[2] // 128
    for z in range(own_ref.shape[0]):
        value = own_ref[z] + other_ref[z]
        peak = jnp.max(jnp.abs(value), axis=0, keepdims=True)
        power = jnp.floor(jnp.log2(jnp.maximum(peak, 2.0**-100))) + 1.0
        code = jnp.round(value * (jnp.exp2(-power) * FULL)).astype(I32).astype(I16)
        for n in range(blocks):
            out_ref[z, n * 64 : (n + 1) * 64] = code[:, n * 128 : (n + 1) * 128]
        powers = [power[:, n * 128 : (n + 1) * 128] for n in range(blocks)]
        powers = jnp.concatenate(powers + [jnp.zeros((16 - blocks, 128), F32)], axis=0)
        out_ref[z, blocks * 64 :] = powers.astype(I32).astype(I16)


def code_sums(own, other):
    columns = own.shape[2]
    rows = columns // 2 + 16
    spec = pl.BlockSpec((2, 64, columns), lambda z: (z, 0, 0))
    return pl.pallas_call(
        code_kernel,
        grid=(4,),
        in_specs=[spec, spec],
        out_specs=pl.BlockSpec((2, rows, 128), lambda z: (z, 0, 0)),
        out_shape=jax.ShapeDtypeStruct((Z, rows, 128), I16),
        cost_estimate=pl.CostEstimate(
            flops=12 * 512 * columns, bytes_accessed=10 * 512 * columns, transcendentals=0
        ),
    )(own, other)


def total_kernel(*refs):
    out_ref = refs[-1]
    for (first, last), ref in zip(CHUNKS, refs[:-1]):
        blocks = 2 * (last - first)
        powers = [ref[z, 64 * blocks :].astype(I32).astype(F32) for z in range(Z)]
        factors = [jnp.exp2(power) * (1.0 / FULL) for power in powers]
        for n in range(blocks):
            total = None
            for z in range(Z):
                code = ref[z, n * 64 : (n + 1) * 64].astype(I32).astype(F32)
                term = code * factors[z][n : n + 1]
                total = term if total is None else total + term
            total = total.reshape(2, 4, 8, 128)
            for i in range(4):
                both = jnp.concatenate([total[0, i], total[1, i]], axis=0)
                half = pl.ds((n % 2) * 128, 128)
                out_ref[i, first + n // 2, :, half] = both.astype(BF16)


def add_up(shares):
    return pl.pallas_call(
        total_kernel, out_shape=jax.ShapeDtypeStruct((4, 4, 16, 256), BF16)
    )(*shares)


def body(amplitudes, integrals, pair_local):
    core = lax.axis_index("core")
    group = lax.axis_index(("z", "core"))
    weights = lax.dynamic_slice_in_dim(pair_local, group * 8, 8, 1)
    masked = integrals * weights.astype(BF16)[:, :, None, None]
    pieces = masked.reshape(4, 8, 8, 16, 16).transpose(3, 0, 2, 1, 4).reshape(16, 32, 128)
    pieces = jnp.broadcast_to(pieces[None], (X, 16, 32, 128)).reshape(64, 32, 128)
    block = lax.all_to_all(pieces, ("x", "z", "core"), 0, 0, tiled=True)
    columns = amplitudes.reshape(16, 8, 4, 16, 256).transpose(2, 0, 1, 3, 4)
    columns = columns.reshape(4, 16, 128, 256)
    block = block.reshape(2048, 128).astype(F32)
    scale, power = raise_to_range(jnp.max(jnp.abs(block)))
    tail = jnp.broadcast_to(power.astype(F16), (16, 128))
    sent = jnp.concatenate([(block * scale).astype(F16), tail])
    received = lax.all_gather(sent, "y", axis=0)
    inverse = lower_again(received[:, -16, 0].astype(F32)).reshape(2, 2, 2)
    w = received[:, :-16].reshape(2, 2, 2, X, 16, 32, 128)
    targets = (1 - core, core)
    halves = [lax.dynamic_index_in_dim(w, c, 1, keepdims=False) for c in targets]
    scales = [lax.dynamic_index_in_dim(inverse, c, 1, keepdims=False) for c in targets]

    def sums(side, j):
        half, scale = halves[side].astype(BF16), scales[side][None, :, :, None, None]
        part = jnp.einsum("psxgrl,glb->xpsrb", half, columns[j], preferred_element_type=F32)
        return (part * scale).reshape(Z, 64, 256)

    shares = []
    for first, last in CHUNKS:
        other, own = (
            jnp.concatenate([sums(side, j) for j in range(first, last)], axis=-1)
            for side in range(2)
        )
        other = lax.ppermute(other, "core", ((0, 1), (1, 0)))
        coded = code_sums(own, other)
        shares.append(lax.all_to_all(coded, "z", 0, 0, tiled=True))
    return add_up(shares)


def solution(mesh):
    chips = Mesh(mesh.devices.reshape(X, Y, Z, 2), ("x", "y", "z", "core"))
    wide, grp = ("x", "y"), ("z", "core")
    in_specs = (P(None, wide, grp, None), P(None, grp, wide, None), P())
    out_specs = P(None, wide, grp, None)
    return jax.shard_map(body, mesh=chips, in_specs=in_specs, out_specs=out_specs, check_vma=False)
```

```python
import jax
import jax.numpy as jnp
from jax import lax
from jax.experimental import pallas as pl
from jax.experimental.pallas import tpu as pltpu
from jax.sharding import Mesh, PartitionSpec as P

BF16, F16, F32, I16, I32 = jnp.bfloat16, jnp.float16, jnp.float32, jnp.int16, jnp.int32
LADDER = (64, 32, 16, 8, 4, 2, 1)
X, Y, Z = 4, 8, 8
FULL = 2.0**14 * 1.875


def raise_to_range(peak):
    peak = jnp.maximum(peak, 2.0**-100)
    scale, power = jnp.ones_like(peak), jnp.zeros_like(peak)
    for step in LADDER:
        fits = peak * scale <= 2.0 ** (15 - step)
        scale = jnp.where(fits, scale * 2.0**step, scale)
        power = jnp.where(fits, power + step, power)
    return scale, power


def lower_again(power):
    scale, left = jnp.ones_like(power), power
    for step in LADDER:
        take = left >= step
        scale = jnp.where(take, scale * 2.0**-step, scale)
        left = jnp.where(take, left - step, left)
    return scale


def cut_kernel(first_ref, pair_ref, in_ref, out_ref):
    lane_block = lax.broadcasted_iota(I32, (8, 128), 1) // 16
    for i in range(4):
        for half in range(2):
            tiles = [
                in_ref[i, k, :, 128 * half : 128 * (half + 1)].astype(F32)
                * pair_ref[i, first_ref[0] + k].astype(F32)
                for k in range(8)
            ]
            for bit in (1, 2, 4):
                low_lanes = (lane_block & bit) == 0
                for k in range(8):
                    if k & bit:
                        continue
                    low, high = tiles[k], tiles[k + bit]
                    tiles[k] = jnp.where(low_lanes, low, pltpu.roll(high, 16 * bit, 1))
                    tiles[k + bit] = jnp.where(
                        low_lanes, pltpu.roll(low, 128 - 16 * bit, 1), high
                    )
            for g in range(8):
                tile = tiles[g].astype(BF16)
                for x in range(X):
                    out_ref[x, 8 * half + g, 8 * i : 8 * (i + 1)] = tile


def cut(first, pair_local, integrals):
    return pl.pallas_call(
        cut_kernel,
        grid_spec=pltpu.PrefetchScalarGridSpec(
            num_scalar_prefetch=2,
            grid=(1,),
            in_specs=[pl.BlockSpec((4, 8, 8, 256), lambda n, f, p: (0, 0, 0, 0))],
            out_specs=pl.BlockSpec((X, 16, 32, 128), lambda n, f, p: (0, 0, 0, 0)),
        ),
        out_shape=jax.ShapeDtypeStruct((X, 16, 32, 128), BF16),
        compiler_params=pltpu.CompilerParams(vmem_limit_bytes=8 << 20),
    )(first, pair_local, integrals)


def code_kernel(own_ref, other_ref, out_ref):
    blocks = own_ref.shape[2] // 128
    for z in range(own_ref.shape[0]):
        value = own_ref[z] + other_ref[z]
        peak = jnp.max(jnp.abs(value), axis=0, keepdims=True)
        power = jnp.floor(jnp.log2(jnp.maximum(peak, 2.0**-100))) + 1.0
        code = jnp.round(value * (jnp.exp2(-power) * FULL)).astype(I32).astype(I16)
        for n in range(blocks):
            out_ref[z, n * 64 : (n + 1) * 64] = code[:, n * 128 : (n + 1) * 128]
        powers = [power[:, n * 128 : (n + 1) * 128] for n in range(blocks)]
        powers = jnp.concatenate(powers + [jnp.zeros((16 - blocks, 128), F32)], axis=0)
        out_ref[z, blocks * 64 :] = powers.astype(I32).astype(I16)


def code_sums(own, other):
    columns = own.shape[2]
    rows = columns // 2 + 16
    spec = pl.BlockSpec((2, 64, columns), lambda z: (z, 0, 0))
    return pl.pallas_call(
        code_kernel,
        grid=(4,),
        in_specs=[spec, spec],
        out_specs=pl.BlockSpec((2, rows, 128), lambda z: (z, 0, 0)),
        out_shape=jax.ShapeDtypeStruct((Z, rows, 128), I16),
        compiler_params=pltpu.CompilerParams(vmem_limit_bytes=12 << 20),
        cost_estimate=pl.CostEstimate(
            flops=12 * 512 * columns, bytes_accessed=10 * 512 * columns, transcendentals=0
        ),
    )(own, other)


def total_kernel(in_ref, out_ref):
    powers = [in_ref[z, 512:].astype(I32).astype(F32) for z in range(Z)]
    factors = [jnp.exp2(power) * (1.0 / FULL) for power in powers]
    for n in range(8):
        total = None
        for z in range(Z):
            code = in_ref[z, n * 64 : (n + 1) * 64].astype(I32).astype(F32)
            term = code * factors[z][n : n + 1]
            total = term if total is None else total + term
        total = total.reshape(2, 4, 8, 128)
        for i in range(4):
            both = jnp.concatenate([total[0, i], total[1, i]], axis=0)
            out_ref[i, n // 2, :, pl.ds((n % 2) * 128, 128)] = both.astype(BF16)


def add_up(shares):
    return pl.pallas_call(
        total_kernel,
        out_shape=jax.ShapeDtypeStruct((4, 4, 16, 256), BF16),
        compiler_params=pltpu.CompilerParams(vmem_limit_bytes=12 << 20),
    )(shares)


def body(amplitudes, integrals, pair_local):
    core = lax.axis_index("core")
    first = 8 * lax.axis_index(("z", "core"))
    pieces = cut(first.reshape(1), pair_local, integrals).reshape(64, 32, 128)
    block = lax.all_to_all(pieces, ("x", "z", "core"), 0, 0, tiled=True)
    columns = amplitudes.reshape(16, 8, 4, 16, 256).transpose(2, 0, 1, 3, 4)
    columns = columns.reshape(4, 16, 128, 256)
    block = block.reshape(2048, 128).astype(F32)
    scale, power = raise_to_range(jnp.max(jnp.abs(block)))
    tail = jnp.broadcast_to(power.astype(F16), (16, 128))
    sent = jnp.concatenate([(block * scale).astype(F16), tail])
    received = lax.all_gather(sent, "y", axis=0)
    inverse = lower_again(received[:, -16, 0].astype(F32)).reshape(2, 2, 2)
    received = received.reshape(2, 2, 2, 2064, 128)
    targets = (1 - core, core)
    scales = [lax.dynamic_index_in_dim(inverse, c, 1, keepdims=False) for c in targets]

    halves = [lax.dynamic_index_in_dim(received, c, 1, keepdims=False) for c in targets]
    halves = lax.optimization_barrier(halves)

    def sums(side, half):
        half = half[:, :, :2048].astype(BF16).reshape(2, 2, X, 16, 32, 128)
        half = lax.optimization_barrier(half)
        scale = scales[side][None, :, :, None, None]
        parts = []
        for j in range(4):
            part = jnp.einsum("psxgrl,glb->xpsrb", half, columns[j], preferred_element_type=F32)
            parts.append((part * scale).reshape(Z, 64, 256))
        return jnp.concatenate(parts, axis=-1)

    other = sums(0, halves[0])
    half, other = lax.optimization_barrier((halves[1], other))
    other = lax.ppermute(other, "core", ((0, 1), (1, 0)))
    coded = code_sums(sums(1, half), other)
    return add_up(lax.all_to_all(coded, "z", 0, 0, tiled=True))


def solution(mesh):
    chips = Mesh(mesh.devices.reshape(X, Y, Z, 2), ("x", "y", "z", "core"))
    wide, grp = ("x", "y"), ("z", "core")
    in_specs = (P(None, wide, grp, None), P(None, grp, wide, None), P())
    out_specs = P(None, wide, grp, None)
    return jax.shard_map(body, mesh=chips, in_specs=in_specs, out_specs=out_specs, check_vma=False)
```

```python
import jax
import jax.numpy as jnp
from jax import lax
from jax.experimental import pallas as pl
from jax.experimental.pallas import tpu as pltpu
from jax.sharding import Mesh, PartitionSpec as P

BF16, F16, F32, I16, I32 = jnp.bfloat16, jnp.float16, jnp.float32, jnp.int16, jnp.int32
LADDER = (64, 32, 16, 8, 4, 2, 1)
X, Y, Z = 4, 8, 8
FULL = 2.0**14 * 1.875


def raise_to_range(peak):
    peak = jnp.maximum(peak, 2.0**-100)
    scale, power = jnp.ones_like(peak), jnp.zeros_like(peak)
    for step in LADDER:
        fits = peak * scale <= 2.0 ** (15 - step)
        scale = jnp.where(fits, scale * 2.0**step, scale)
        power = jnp.where(fits, power + step, power)
    return scale, power


def lower_again(power):
    scale, left = jnp.ones_like(power), power
    for step in LADDER:
        take = left >= step
        scale = jnp.where(take, scale * 2.0**-step, scale)
        left = jnp.where(take, left - step, left)
    return scale


def cut_kernel(first_ref, pair_ref, in_ref, out_ref):
    lane_block = lax.broadcasted_iota(I32, (8, 128), 1) // 16
    for i in range(4):
        for half in range(2):
            tiles = [
                in_ref[i, k, :, 128 * half : 128 * (half + 1)].astype(F32)
                * pair_ref[i, first_ref[0] + k].astype(F32)
                for k in range(8)
            ]
            for bit in (1, 2, 4):
                low_lanes = (lane_block & bit) == 0
                for k in range(8):
                    if k & bit:
                        continue
                    low, high = tiles[k], tiles[k + bit]
                    tiles[k] = jnp.where(low_lanes, low, pltpu.roll(high, 16 * bit, 1))
                    tiles[k + bit] = jnp.where(
                        low_lanes, pltpu.roll(low, 128 - 16 * bit, 1), high
                    )
            for g in range(8):
                tile = tiles[g].astype(BF16)
                for x in range(X):
                    out_ref[x, 8 * half + g, 8 * i : 8 * (i + 1)] = tile


def cut(first, pair_local, integrals):
    return pl.pallas_call(
        cut_kernel,
        grid_spec=pltpu.PrefetchScalarGridSpec(
            num_scalar_prefetch=2,
            grid=(1,),
            in_specs=[pl.BlockSpec((4, 8, 8, 256), lambda n, f, p: (0, 0, 0, 0))],
            out_specs=pl.BlockSpec((X, 16, 32, 128), lambda n, f, p: (0, 0, 0, 0)),
        ),
        out_shape=jax.ShapeDtypeStruct((X, 16, 32, 128), BF16),
    )(first, pair_local, integrals)


def code_kernel(own_ref, other_ref, out_ref):
    blocks = own_ref.shape[2] // 128
    for z in range(own_ref.shape[0]):
        value = own_ref[z] + other_ref[z]
        peak = jnp.max(jnp.abs(value), axis=0, keepdims=True)
        power = jnp.floor(jnp.log2(jnp.maximum(peak, 2.0**-100))) + 1.0
        code = jnp.round(value * (jnp.exp2(-power) * FULL)).astype(I32).astype(I16)
        for n in range(blocks):
            out_ref[z, n * 64 : (n + 1) * 64] = code[:, n * 128 : (n + 1) * 128]
        powers = [power[:, n * 128 : (n + 1) * 128] for n in range(blocks)]
        powers = jnp.concatenate(powers + [jnp.zeros((16 - blocks, 128), F32)], axis=0)
        out_ref[z, blocks * 64 :] = powers.astype(I32).astype(I16)


def code_sums(own, other):
    columns = own.shape[2]
    rows = columns // 2 + 16
    spec = pl.BlockSpec((2, 64, columns), lambda z: (z, 0, 0))
    return pl.pallas_call(
        code_kernel,
        grid=(4,),
        in_specs=[spec, spec],
        out_specs=pl.BlockSpec((2, rows, 128), lambda z: (z, 0, 0)),
        out_shape=jax.ShapeDtypeStruct((Z, rows, 128), I16),
        compiler_params=pltpu.CompilerParams(vmem_limit_bytes=12 << 20),
        cost_estimate=pl.CostEstimate(
            flops=12 * 512 * columns, bytes_accessed=10 * 512 * columns, transcendentals=0
        ),
    )(own, other)


def total_kernel(in_ref, out_ref):
    powers = [in_ref[z, 512:].astype(I32).astype(F32) for z in range(Z)]
    factors = [jnp.exp2(power) * (1.0 / FULL) for power in powers]
    for n in range(8):
        total = None
        for z in range(Z):
            code = in_ref[z, n * 64 : (n + 1) * 64].astype(I32).astype(F32)
            term = code * factors[z][n : n + 1]
            total = term if total is None else total + term
        total = total.reshape(2, 4, 8, 128)
        for i in range(4):
            both = jnp.concatenate([total[0, i], total[1, i]], axis=0)
            out_ref[i, n // 2, :, pl.ds((n % 2) * 128, 128)] = both.astype(BF16)


def add_up(shares):
    return pl.pallas_call(
        total_kernel,
        out_shape=jax.ShapeDtypeStruct((4, 4, 16, 256), BF16),
        compiler_params=pltpu.CompilerParams(vmem_limit_bytes=12 << 20),
    )(shares)


def body(amplitudes, integrals, pair_local):
    core = lax.axis_index("core")
    first = 8 * lax.axis_index(("z", "core"))
    pieces = cut(first.reshape(1), pair_local, integrals).reshape(64, 32, 128)
    block = lax.all_to_all(pieces, ("x", "z", "core"), 0, 0, tiled=True)
    columns = amplitudes.reshape(16, 8, 4, 16, 256).transpose(2, 0, 1, 3, 4)
    columns = columns.reshape(4, 16, 128, 256)
    block = block.reshape(2048, 128).astype(F32)
    scale, power = raise_to_range(jnp.max(jnp.abs(block)))
    tail = jnp.broadcast_to(power.astype(F16), (16, 128))
    sent = jnp.concatenate([(block * scale).astype(F16), tail])
    received = lax.all_gather(sent, "y", axis=0)
    received = received.reshape(2, 2, 2, 2064, 128)
    targets = (1 - core, core)
    halves = [lax.dynamic_index_in_dim(received, c, 1, keepdims=False) for c in targets]
    halves = lax.optimization_barrier(halves)

    def sums(side, cuts):
        scale = lower_again(halves[side][:, :, 2048, 0].astype(F32))[None, :, :, None, None]
        parts = []
        for cut_columns in cuts:
            half, *some = lax.optimization_barrier((halves[side], *(columns[j] for j in cut_columns)))
            half = half[:, :, :2048].astype(BF16).reshape(2, 2, X, 16, 32, 128)
            for column in some:
                part = jnp.einsum("psxgrl,glb->xpsrb", half, column, preferred_element_type=F32)
                parts.append((part * scale).reshape(Z, 64, 256))
        return jnp.concatenate(parts, axis=-1)

    other = lax.ppermute(sums(0, ((0,), (1,), (2, 3))), "core", ((0, 1), (1, 0)))
    coded = code_sums(sums(1, ((0, 1, 2, 3),)), other)
    return add_up(lax.all_to_all(coded, "z", 0, 0, tiled=True))


def solution(mesh):
    chips = Mesh(mesh.devices.reshape(X, Y, Z, 2), ("x", "y", "z", "core"))
    wide, grp = ("x", "y"), ("z", "core")
    in_specs = (P(None, wide, grp, None), P(None, grp, wide, None), P())
    out_specs = P(None, wide, grp, None)
    return jax.shard_map(body, mesh=chips, in_specs=in_specs, out_specs=out_specs, check_vma=False)
```

```python
import jax
import jax.numpy as jnp
from jax import lax
from jax.experimental import pallas as pl
from jax.experimental.pallas import tpu as pltpu
from jax.sharding import Mesh, PartitionSpec as P

BF16, F16, F32, I16, I32 = jnp.bfloat16, jnp.float16, jnp.float32, jnp.int16, jnp.int32
LADDER = (64, 32, 16, 8, 4, 2, 1)
X, Y, Z = 4, 8, 8
FULL = 2.0**14 * 1.875


def raise_to_range(peak):
    peak = jnp.maximum(peak, 2.0**-100)
    scale, power = jnp.ones_like(peak), jnp.zeros_like(peak)
    for step in LADDER:
        fits = peak * scale <= 2.0 ** (15 - step)
        scale = jnp.where(fits, scale * 2.0**step, scale)
        power = jnp.where(fits, power + step, power)
    return scale, power


def lower_again(power):
    scale, left = jnp.ones_like(power), power
    for step in LADDER:
        take = left >= step
        scale = jnp.where(take, scale * 2.0**-step, scale)
        left = jnp.where(take, left - step, left)
    return scale


def cut_kernel(first_ref, pair_ref, in_ref, out_ref):
    lane_block = lax.broadcasted_iota(I32, (8, 128), 1) // 16
    for i in range(4):
        for half in range(2):
            tiles = [
                in_ref[i, k, :, 128 * half : 128 * (half + 1)].astype(F32)
                * pair_ref[i, first_ref[0] + k].astype(F32)
                for k in range(8)
            ]
            for bit in (1, 2, 4):
                low_lanes = (lane_block & bit) == 0
                for k in range(8):
                    if k & bit:
                        continue
                    low, high = tiles[k], tiles[k + bit]
                    tiles[k] = jnp.where(low_lanes, low, pltpu.roll(high, 16 * bit, 1))
                    tiles[k + bit] = jnp.where(
                        low_lanes, pltpu.roll(low, 128 - 16 * bit, 1), high
                    )
            for g in range(8):
                tile = tiles[g].astype(BF16)
                out_ref[8 * half + g, 8 * i : 8 * (i + 1)] = tile


def cut(first, pair_local, integrals):
    return pl.pallas_call(
        cut_kernel,
        grid_spec=pltpu.PrefetchScalarGridSpec(
            num_scalar_prefetch=2,
            grid=(1,),
            in_specs=[pl.BlockSpec((4, 8, 8, 256), lambda n, f, p: (0, 0, 0, 0))],
            out_specs=pl.BlockSpec((16, 32, 128), lambda n, f, p: (0, 0, 0)),
        ),
        out_shape=jax.ShapeDtypeStruct((16, 32, 128), BF16),
    )(first, pair_local, integrals)


def code_kernel(own_ref, other_ref, out_ref):
    blocks = own_ref.shape[2] // 128
    for z in range(own_ref.shape[0]):
        value = own_ref[z] + other_ref[z]
        peak = jnp.max(jnp.abs(value), axis=0, keepdims=True)
        power = jnp.floor(jnp.log2(jnp.maximum(peak, 2.0**-100))) + 1.0
        code = jnp.round(value * (jnp.exp2(-power) * FULL)).astype(I32).astype(I16)
        for n in range(blocks):
            out_ref[z, n * 64 : (n + 1) * 64] = code[:, n * 128 : (n + 1) * 128]
        powers = [power[:, n * 128 : (n + 1) * 128] for n in range(blocks)]
        powers = jnp.concatenate(powers + [jnp.zeros((16 - blocks, 128), F32)], axis=0)
        out_ref[z, blocks * 64 :] = powers.astype(I32).astype(I16)


def code_sums(own, other):
    columns = own.shape[2]
    rows = columns // 2 + 16
    spec = pl.BlockSpec((2, 64, columns), lambda z: (z, 0, 0))
    return pl.pallas_call(
        code_kernel,
        grid=(4,),
        in_specs=[spec, spec],
        out_specs=pl.BlockSpec((2, rows, 128), lambda z: (z, 0, 0)),
        out_shape=jax.ShapeDtypeStruct((Z, rows, 128), I16),
        compiler_params=pltpu.CompilerParams(vmem_limit_bytes=12 << 20),
        cost_estimate=pl.CostEstimate(
            flops=12 * 512 * columns, bytes_accessed=10 * 512 * columns, transcendentals=0
        ),
    )(own, other)


def total_kernel(in_ref, out_ref):
    powers = [in_ref[z, 512:].astype(I32).astype(F32) for z in range(Z)]
    factors = [jnp.exp2(power) * (1.0 / FULL) for power in powers]
    for n in range(8):
        total = None
        for z in range(Z):
            code = in_ref[z, n * 64 : (n + 1) * 64].astype(I32).astype(F32)
            term = code * factors[z][n : n + 1]
            total = term if total is None else total + term
        total = total.reshape(2, 4, 8, 128)
        for i in range(4):
            both = jnp.concatenate([total[0, i], total[1, i]], axis=0)
            out_ref[i, n // 2, :, pl.ds((n % 2) * 128, 128)] = both.astype(BF16)


def add_up(shares):
    return pl.pallas_call(
        total_kernel,
        out_shape=jax.ShapeDtypeStruct((4, 4, 16, 256), BF16),
        compiler_params=pltpu.CompilerParams(vmem_limit_bytes=12 << 20),
    )(shares)


def body(amplitudes, integrals, pair_local):
    core = lax.axis_index("core")
    first = 8 * lax.axis_index(("z", "core"))
    pieces = cut(first.reshape(1), pair_local, integrals)
    block = lax.all_to_all(pieces, ("z", "core"), 0, 0, tiled=True)
    columns = amplitudes.reshape(16, 8, 4, 16, 256).transpose(2, 0, 1, 3, 4)
    columns = columns.reshape(4, 16, 128, 256)
    block = block.reshape(512, 128).astype(F32)
    scale, power = raise_to_range(jnp.max(jnp.abs(block)))
    tail = jnp.broadcast_to(power.astype(F16), (8, 128))
    sent = jnp.concatenate([(block * scale).astype(F16), tail])
    received = lax.all_gather(sent, ("y", "x"), axis=0)
    received = received.reshape(2, 2, 2, X, 520, 128)
    targets = (1 - core, core)
    halves = [lax.dynamic_index_in_dim(received, c, 1, keepdims=False) for c in targets]
    halves = lax.optimization_barrier(halves)

    def sums(side, cuts):
        scale = lower_again(halves[side][:, :, :, 512, 0].astype(F32)).transpose(2, 0, 1)[..., None, None]
        parts = {}
        for cut_columns in cuts:
            some = [columns[j] for j in cut_columns]
            earlier = [parts[j] for j in parts]
            half, some, earlier = lax.optimization_barrier((halves[side], some, earlier))
            parts = dict(zip(parts, earlier))
            half = half[:, :, :, :512].astype(BF16).reshape(2, 2, X, 16, 32, 128)
            for j, column in zip(cut_columns, some):
                part = jnp.einsum("psxgrl,glb->xpsrb", half, column, preferred_element_type=F32)
                parts[j] = (part * scale).reshape(Z, 64, 256)
        return jnp.concatenate([parts[j] for j in range(4)], axis=-1)

    other = lax.ppermute(sums(0, ((2, 3), (0, 1))), "core", ((0, 1), (1, 0)))
    coded = code_sums(sums(1, ((0, 1, 2, 3),)), other)
    return add_up(lax.all_to_all(coded, "z", 0, 0, tiled=True))


def solution(mesh):
    chips = Mesh(mesh.devices.reshape(X, Y, Z, 2), ("x", "y", "z", "core"))
    wide, grp = ("x", "y"), ("z", "core")
    in_specs = (P(None, wide, grp, None), P(None, grp, wide, None), P())
    out_specs = P(None, wide, grp, None)
    return jax.shard_map(body, mesh=chips, in_specs=in_specs, out_specs=out_specs, check_vma=False)
```
